32 devices in a mesh: row: 2 (over core), col: 4 (over y, x), depth: 4 (over z).
Axes of the slice: x: 2, y: 2, z: 4, core: 2. Of those that a mesh axis runs over, the one named last changes fastest.
Arguments:
- head_rhs: float32 [2, 1024, 4096], P(None, 'row', ('col', 'depth')), may hold values from -6 to 6
- head_factor: float32 [1024, 1024], P('row', 'depth'), may hold values from -0.09375 to 0.09375
- inverses: float32 [2, 1024, 1024], P(None, 'depth'), as said below
- trail_factor: float32 [512, 2, 1024], P('row', None, 'depth'), may hold values from -0.125 to 0.125
- trail_rhs: float32 [512, 4096], P('row', ('col', 'depth')), may hold values from -6 to 6
Outputs:
- solution: float32 [2, 1024, 4096], P(None, 'depth', 'col')
- trail_out: float32 [512, 4096], P('row', ('col', 'depth'))
The draws below stay inside these ranges and needn't reach their ends.
Inputs may be any that keep to these rules, and one draw needn't show every extreme that they name: `inverses`: each of the two blocks is lower triangular with a positive diagonal.
All inputs are finite; a program needn't handle non-finite values.
Results may differ from the reference program's by a relative error of at most 0.00009.
Values sent between devices are 32-bit elements; how exact they have to be, the bound alone decides.
No kernel may reach another device: no remote copies, remote signals or barrier semaphores. Data moves between devices by JAX's collectives and lax.ppermute only.
A program may use at most 64 MiB of HBM per device.

```python
import jax
import jax.numpy as jnp
from jax import lax

NB = 1024
COLS = 4096
TRAIL = 512


def draw_inverses(key, part):
    first_key, second_key = jax.random.split(jax.random.fold_in(key, 11), 2)
    diagonal = jax.random.uniform(first_key, (2, NB), jnp.float32, 1.0, 2.0)
    lower = jax.random.normal(second_key, (2, NB, NB), jnp.float32) / jnp.sqrt(jnp.float32(NB))
    rows = jnp.arange(NB)[:, None]
    columns = jnp.arange(NB)[None, :]
    strict = (rows > columns)[None, :, :]
    identity = (rows == columns).astype(jnp.float32)[None, :, :]
    return jnp.where(strict, lower, 0.0) + identity * diagonal[:, :, None]


def block_scale(rng, shape, cuts, least, top_value):
    gain = 1.0
    for dim, shards_of in cuts:
        draws = jax.random.uniform(jax.random.fold_in(jax.random.fold_in(rng, 6), dim), (shards_of,), jnp.float32, least / len(cuts), top_value / len(cuts))
        gain = gain * jnp.repeat(jnp.exp(draws), shape[dim] // shards_of).reshape((-1,) + (1,) * (len(shape) - 1 - dim))
    return gain


def noise(rng, extent, scale, limit, cuts=(), kind=jnp.bfloat16):
    values = scale * jax.random.normal(rng, extent, jnp.float32)
    if cuts:
        values = values * block_scale(rng, extent, cuts, -0.22, 0.18)
    return jnp.clip(values, -limit, limit).astype(kind)


def setup_inputs(seed: int = 0) -> dict:
    streams_of = jax.random.split(jax.random.key(seed), 6)
    return {
        "head_rhs": noise(streams_of[0], (2, NB, COLS), 1.0, 6.0, ((1, 2), (2, 16)), jnp.float32),
        "head_factor": noise(streams_of[1], (NB, NB), (4 * NB) ** -0.5, 0.09375, ((0, 2), (1, 4)), jnp.float32),
        "inverses": draw_inverses(jax.random.fold_in(streams_of[5], 71), 0),
        "trail_factor": noise(streams_of[3], (TRAIL, 2, NB), (2 * NB) ** -0.5, 0.125, ((0, 2), (2, 4)), jnp.float32),
        "trail_rhs": noise(streams_of[4], (TRAIL, COLS), 1.0, 6.0, ((0, 2), (1, 16)), jnp.float32),
    }


def product(left, right):
    return jnp.dot(left, right, precision=lax.Precision.HIGHEST, preferred_element_type=jnp.float32)


def reference(head_rhs, head_factor, inverses, trail_factor, trail_rhs):
    solved_first = product(inverses[0], head_rhs[0])
    second_rhs = head_rhs[1] - product(head_factor, solved_first)
    trail_mid = trail_rhs - product(trail_factor[:, 0, :], solved_first)
    solved_second = product(inverses[1], second_rhs)
    trail_out = trail_mid - product(trail_factor[:, 1, :], solved_second)
    return jnp.stack([solved_first, solved_second]), trail_out
```

```python
import jax
import jax.numpy as jnp
from jax import lax
from jax.sharding import PartitionSpec as P


def product(left, right):
    return jnp.dot(left, right, precision=lax.Precision.HIGH, preferred_element_type=jnp.float32)


def exchange(value, axis, flip):
    size = lax.axis_size(axis)
    return lax.ppermute(value, axis, [(i, i ^ flip) for i in range(size)])


def in_order(blocks, index):
    bit = 1
    while bit < len(blocks):
        odd = (index & bit) != 0
        blocks = [jnp.where(odd, blocks[k ^ bit], blocks[k]) for k in range(len(blocks))]
        bit *= 2
    return blocks


def share_rows(value, dim):
    size = lax.axis_size("row")
    index = lax.axis_index("row")
    bit = 1
    while bit < size:
        other = exchange(value, "row", bit)
        odd = (index & bit) != 0
        value = jnp.concatenate([jnp.where(odd, other, value), jnp.where(odd, value, other)], axis=dim)
        bit *= 2
    return value


def own_part(value, dim, axis):
    size = value.shape[dim] // lax.axis_size(axis)
    return lax.dynamic_slice_in_dim(value, lax.axis_index(axis) * size, size, dim)


def from_depth(part):
    return jnp.stack([exchange(part, "depth", k) for k in range(1, lax.axis_size("depth"))])


def from_columns(parts, first):
    index = lax.axis_index("col")
    size = lax.axis_size("col")
    known = {0: parts}
    bits = []
    bit = 1
    while bit < size:
        bits.append(bit)
        bit *= 2
    for bit in bits:
        known[bit] = exchange(parts, "col", bit)
    order = bits if first else bits[::-1]
    for k in range(1, size):
        if k in known:
            continue
        last = [b for b in order if k & b][-1]
        known[k] = exchange(known[k ^ last], "col", last)
    return in_order([known[k] for k in range(size)], index)


def gather_factor(own, dim, first):
    parts = from_depth(own_part(own, dim, "col"))
    parts = from_columns(parts, first)
    rest = jnp.concatenate(parts, axis=dim + 1)
    return [own] + [rest[k] for k in range(rest.shape[0])]


def to_output(block_parts):
    arrived = [block_parts[0]] + [exchange(block_parts[k], "depth", k) for k in range(1, len(block_parts))]
    return jnp.concatenate(in_order(arrived, lax.axis_index("depth")), axis=1)


def on_device(head_rhs, head_factor, inverses, trail_factor, trail_rhs):
    lower = own_part(inverses, 1, "row")
    first_inverse = gather_factor(lower[0], 0, True)
    factor = gather_factor(head_factor, 0, False)
    second_inverse = gather_factor(lower[1], 0, True)
    trail = gather_factor(trail_factor, 0, False)

    count = len(factor)
    rows = lower.shape[1]
    rhs = share_rows(head_rhs[0], 0)
    first_parts = [product(piece, rhs) for piece in first_inverse]
    first_out = to_output(first_parts)
    first = share_rows(jnp.stack(first_parts), 1)
    change = sum(product(factor[k], first[k]) for k in range(count))
    second_rhs = share_rows(head_rhs[1] - change, 0)
    second_parts = [product(piece, second_rhs) for piece in second_inverse]
    second_out = to_output(second_parts)
    second = share_rows(jnp.stack(second_parts), 1)
    trail_out = trail_rhs - sum(product(trail[k][:, 0, :], first[k]) for k in range(count))
    trail_out = trail_out - sum(product(trail[k][:, 1, :], second[k]) for k in range(count))
    return share_rows(jnp.stack([first_out, second_out]), 1), trail_out


def solution(mesh):
    placed = (
        P(None, "row", ("col", "depth")),
        P("row", "depth"),
        P(None, "depth", None),
        P("row", None, "depth"),
        P("row", ("col", "depth")),
    )
    return jax.shard_map(
        on_device,
        mesh=mesh,
        in_specs=placed,
        out_specs=(P(None, "depth", "col"), P("row", ("col", "depth"))),
        check_vma=False,
    )
```

```python
import jax
import jax.numpy as jnp
from jax import lax
from jax.sharding import PartitionSpec as P


def product(left, right):
    return jnp.dot(left, right, precision=lax.Precision.HIGH, preferred_element_type=jnp.float32)


def exchange(value, axis, flip):
    size = lax.axis_size(axis)
    return lax.ppermute(value, axis, [(i, i ^ flip) for i in range(size)])


def in_order(blocks, index):
    bit = 1
    while bit < len(blocks):
        odd = (index & bit) != 0
        blocks = [jnp.where(odd, blocks[k ^ bit], blocks[k]) for k in range(len(blocks))]
        bit *= 2
    return blocks


def share_rows(value, dim):
    size = lax.axis_size("row")
    index = lax.axis_index("row")
    bit = 1
    while bit < size:
        other = exchange(value, "row", bit)
        odd = (index & bit) != 0
        value = jnp.concatenate([jnp.where(odd, other, value), jnp.where(odd, value, other)], axis=dim)
        bit *= 2
    return value


def own_part(value, dim, axis):
    size = value.shape[dim] // lax.axis_size(axis)
    return lax.dynamic_slice_in_dim(value, lax.axis_index(axis) * size, size, dim)


def from_depth(part):
    return jnp.stack([exchange(part, "depth", k) for k in range(1, lax.axis_size("depth"))])


def from_columns(parts, first):
    index = lax.axis_index("col")
    size = lax.axis_size("col")
    known = {0: parts}
    bits = []
    bit = 1
    while bit < size:
        bits.append(bit)
        bit *= 2
    for bit in bits:
        known[bit] = exchange(parts, "col", bit)
    order = bits if first else bits[::-1]
    for k in range(1, size):
        if k in known:
            continue
        last = [b for b in order if k & b][-1]
        known[k] = exchange(known[k ^ last], "col", last)
    return in_order([known[k] for k in range(size)], index)


def gather_factor(own, dim, first):
    parts = from_depth(own_part(own, dim, "col"))
    parts = from_columns(parts, first)
    rest = jnp.concatenate(parts, axis=dim + 1)
    return [own] + [rest[k] for k in range(rest.shape[0])]


def to_output(block_parts):
    arrived = [block_parts[0]] + [exchange(block_parts[k], "depth", k) for k in range(1, len(block_parts))]
    return jnp.concatenate(in_order(arrived, lax.axis_index("depth")), axis=1)


def steps(head_rhs, head_factor, inverses, trail_factor, trail_rhs):
    lower = own_part(inverses, 1, "row")
    first_inverse = gather_factor(lower[0], 0, True)
    factor = gather_factor(head_factor, 0, False)
    second_inverse = gather_factor(lower[1], 0, True)
    trail = gather_factor(trail_factor, 0, False)

    count = len(factor)
    rhs = share_rows(head_rhs[0], 0)
    first_parts = [product(piece, rhs) for piece in first_inverse]
    first_out = to_output(first_parts)
    first = share_rows(jnp.stack(first_parts), 1)
    change = sum(product(factor[k], first[k]) for k in range(count))
    second_rhs = share_rows(head_rhs[1] - change, 0)
    second_parts = [product(piece, second_rhs) for piece in second_inverse]
    second_out = to_output(second_parts)
    second = share_rows(jnp.stack(second_parts), 1)
    trail_out = trail_rhs - sum(product(trail[k][:, 0, :], first[k]) for k in range(count))
    trail_out = trail_out - sum(product(trail[k][:, 1, :], second[k]) for k in range(count))
    return share_rows(jnp.stack([first_out, second_out]), 1), trail_out


def solution(mesh):
    placed = (
        P(None, "row", ("col", "depth")),
        P("row", "depth"),
        P(None, "depth", None),
        P("row", None, "depth"),
        P("row", ("col", "depth")),
    )
    return jax.shard_map(
        steps,
        mesh=mesh,
        in_specs=placed,
        out_specs=(P(None, "depth", "col"), P("row", ("col", "depth"))),
        check_vma=False,
    )
```

```python
import functools

import jax
import jax.numpy as jnp
from jax import lax
from jax.experimental import pallas as pl
from jax.experimental.pallas import tpu as pltpu
from jax.sharding import PartitionSpec as P


def exchange(value, axis, flip):
    pairs = [(i, i ^ flip) for i in range(lax.axis_size(axis))]
    return lax.ppermute(value, axis, pairs)


def in_order(blocks, index):
    bit = 1
    while bit < len(blocks):
        odd = (index & bit) != 0
        blocks = [jnp.where(odd, blocks[k ^ bit], blocks[k]) for k in range(len(blocks))]
        bit *= 2
    return blocks


def share_rows(value, dim):
    index = lax.axis_index("row")
    bit = 1
    while bit < lax.axis_size("row"):
        other = exchange(value, "row", bit)
        odd = (index & bit) != 0
        value = jnp.concatenate([jnp.where(odd, other, value), jnp.where(odd, value, other)], axis=dim)
        bit *= 2
    return value


def own_part(value, dim, axis):
    size = value.shape[dim] // lax.axis_size(axis)
    return lax.dynamic_slice_in_dim(value, lax.axis_index(axis) * size, size, dim)


def from_depth(part, relay):
    size = lax.axis_size("depth")
    if not (relay and size == 4):
        return jnp.stack([exchange(part, "depth", k) for k in range(1, size)])
    near = exchange(part, "depth", 1)
    across = lax.ppermute(jnp.stack([part, near]), "depth", [(1, 2), (2, 1)])
    handed = lax.ppermute(across, "depth", [(1, 0), (2, 3)])
    index = lax.axis_index("depth")
    outer = (index == 0) | (index == size - 1)
    far = [jnp.where(outer, handed[0], across[1]), jnp.where(outer, handed[1], across[0])]
    return jnp.stack([near] + far)


def from_columns(parts, low_first):
    size = lax.axis_size("col")
    bits = [1 << b for b in range(size.bit_length() - 1)]
    known = {0: parts}
    for bit in bits:
        known[bit] = exchange(parts, "col", bit)
    for k in range(1, size):
        if k not in known:
            via = [b for b in (bits if low_first else bits[::-1]) if k & b][-1]
            known[k] = exchange(known[k ^ via], "col", via)
    return [known[k] for k in range(size)]


def gather_factor(own, low_first, relay):
    return from_columns(from_depth(own_part(own, 0, "col"), relay), low_first)


def halves(value):
    high = value.astype(jnp.bfloat16)
    return high, (value - high.astype(jnp.float32)).astype(jnp.bfloat16)


def product(left, right):
    left_high, left_low = halves(left)
    right_high, right_low = right
    dot = functools.partial(jnp.dot, preferred_element_type=jnp.float32)
    return dot(left_high, right_high) + (dot(left_high, right_low) + dot(left_low, right_high))


def solve_kernel(place, own, *rest):
    *parts, rhs, out = rest
    right = halves(rhs[...])
    count, size, depth = parts[0].shape
    out[0] = product(own[0], right)
    left = jnp.concatenate([part[...].reshape(count * size, depth) for part in parts])
    rows = product(left, right)
    for k in range(len(parts)):
        at = pl.multiple_of((place[1] ^ k) * size, size)
        for j in range(count):
            from_row = (k * count + j) * size
            out[j + 1, pl.ds(at, size), :] = rows[from_row : from_row + size]


def update_kernel(quarters, place, own, *rest):
    *solved, base, out = rest[quarters:]
    parts = rest[:quarters]
    count, size, _ = parts[0].shape
    depth = solved[0].shape[1]
    near = far = None
    for s, blocks in enumerate(solved):
        at = slice(s * depth, (s + 1) * depth)
        for j in range(count + 1):
            right = halves(blocks[j])
            if j == 0:
                term = product(own[:, at], right)
                near = term if near is None else near + term
            else:
                left = jnp.concatenate([part[j - 1][:, at] for part in parts])
                term = product(left, right)
                far = term if far is None else far + term
    out[...] = base[...] - near
    for k in range(quarters):
        at = pl.ds(pl.multiple_of((place[1] ^ k) * size, size), size)
        out[at, :] = out[at, :] - far[k * size : (k + 1) * size]


def whole(array):
    zeros = (0,) * array.ndim
    return pl.BlockSpec(array.shape, lambda i, p: zeros)


def cost(flops, arrays):
    moved = sum(4 * a.size for a in arrays)
    return pl.CostEstimate(flops=flops, bytes_accessed=moved, transcendentals=0)


def call_kernel(kernel, place, first_spec, operands, shape, flops):
    out = jax.ShapeDtypeStruct(shape, jnp.float32)
    return pl.pallas_call(
        kernel,
        out_shape=out,
        grid_spec=pltpu.PrefetchScalarGridSpec(
            num_scalar_prefetch=1,
            grid=(1,),
            in_specs=[first_spec] + [whole(a) for a in operands[1:]],
            out_specs=whole(out),
        ),
        cost_estimate=cost(flops, operands[1:]),
    )(place, *operands)


def plain_product(left, right):
    return jnp.dot(left, right, precision=lax.Precision.HIGH, preferred_element_type=jnp.float32)


def solve(place, section, inverses, parts, rhs):
    rows = inverses.shape[1] // lax.axis_size("row")
    nb, cols = rhs.shape
    count, size, _ = parts[0].shape
    if size % 8:
        own = plain_product(own_part(inverses[section], 0, "row"), rhs)
        ordered = jnp.concatenate(in_order(list(parts), place[1]), axis=1)
        return jnp.stack([own] + [plain_product(ordered[j], rhs) for j in range(count)])
    spec = pl.BlockSpec((1, rows, nb), lambda i, p: (section, p[0], 0))
    shape = (count + 1, rows, cols)
    flops = 6 * (count + 1) * rows * nb * cols
    return call_kernel(solve_kernel, place, spec, (inverses, *parts, rhs), shape, flops)


def update(place, own, parts, solved, base):
    count, size, _ = parts[0].shape
    depth = solved[0].shape[1]
    if size % 8:
        ordered = jnp.concatenate(in_order(list(parts), place[1]), axis=1)
        for s, blocks in enumerate(solved):
            at = slice(s * depth, (s + 1) * depth)
            base = base - plain_product(own[:, at], blocks[0])
            for j in range(count):
                base = base - plain_product(ordered[j][:, at], blocks[j + 1])
        return base
    kernel = functools.partial(update_kernel, len(parts))
    flops = 6 * own.size * (count + 1) * base.shape[1]
    return call_kernel(kernel, place, whole(own), (own, *parts, *solved, base), base.shape, flops)


def to_output(parts):
    arrived = [parts[0]]
    for k in range(1, parts.shape[0]):
        arrived.append(exchange(parts[k], "depth", k))
    placed = jnp.concatenate(in_order(arrived, lax.axis_index("depth")), axis=1)
    return share_rows(placed, 0)


def steps(head_rhs, head_factor, inverses, trail_factor, trail_rhs):
    place = jnp.stack([lax.axis_index("row"), lax.axis_index("col")])
    lower = own_part(inverses, 1, "row")
    count = trail_factor.shape[0]
    trail_own = trail_factor.reshape(count, -1)
    trail_part = own_part(trail_factor, 0, "col").reshape(count // lax.axis_size("col"), -1)
    first_factor = gather_factor(lower[0], True, False)
    mid_factor = gather_factor(head_factor, False, True)
    second_factor = gather_factor(lower[1], True, True)
    trail_parts = from_columns(from_depth(trail_part, True), False)

    rhs = share_rows(head_rhs[0], 0)
    first_part = solve(place, 0, inverses, first_factor, rhs)
    first = share_rows(first_part, 1)
    second_rhs = update(place, head_factor, mid_factor, [first], head_rhs[1])
    second_rhs = share_rows(second_rhs, 0)
    second_part = solve(place, 1, inverses, second_factor, second_rhs)
    second = share_rows(second_part, 1)
    trail_out = update(place, trail_own, trail_parts, [first, second], trail_rhs)
    return jnp.stack([to_output(first_part), to_output(second_part)]), trail_out


def solution(mesh):
    placed = (
        P(None, "row", ("col", "depth")),
        P("row", "depth"),
        P(None, "depth", None),
        P("row", None, "depth"),
        P("row", ("col", "depth")),
    )
    return jax.shard_map(
        steps,
        mesh=mesh,
        in_specs=placed,
        out_specs=(P(None, "depth", "col"), P("row", ("col", "depth"))),
        check_vma=False,
    )
```

```python
import functools

import jax
import jax.numpy as jnp
from jax import lax
from jax.experimental import pallas as pl
from jax.experimental.pallas import tpu as pltpu
from jax.sharding import PartitionSpec as P


def exchange(value, axis, flip):
    pairs = [(i, i ^ flip) for i in range(lax.axis_size(axis))]
    return lax.ppermute(value, axis, pairs)


def in_order(blocks, index):
    bit = 1
    while bit < len(blocks):
        odd = (index & bit) != 0
        blocks = [jnp.where(odd, blocks[k ^ bit], blocks[k]) for k in range(len(blocks))]
        bit *= 2
    return blocks


def share_rows(value, dim):
    index = lax.axis_index("row")
    bit = 1
    while bit < lax.axis_size("row"):
        other = exchange(value, "row", bit)
        odd = (index & bit) != 0
        value = jnp.concatenate([jnp.where(odd, other, value), jnp.where(odd, value, other)], axis=dim)
        bit *= 2
    return value


def own_part(value, dim, axis):
    size = value.shape[dim] // lax.axis_size(axis)
    return lax.dynamic_slice_in_dim(value, lax.axis_index(axis) * size, size, dim)


def from_depth(part, relay):
    size = lax.axis_size("depth")
    if not (relay and size == 4):
        parts = [exchange(part, "depth", k) for k in range(1, size)]
        return jnp.stack(parts)
    near = exchange(part, "depth", 1)
    across = lax.ppermute(jnp.stack([part, near]), "depth", [(1, 2), (2, 1)])
    handed = lax.ppermute(across, "depth", [(1, 0), (2, 3)])
    index = lax.axis_index("depth")
    outer = (index == 0) | (index == size - 1)
    far = [jnp.where(outer, handed[0], across[1]), jnp.where(outer, handed[1], across[0])]
    return jnp.stack([near] + far)


def pack_lower(parts):
    index = lax.axis_index("depth")
    size = len(parts) + 1
    packed = []
    for n in range(1, size):
        pick = None
        for d in range(size):
            source = n - 1 if n - 1 < d else n
            part = parts[(source ^ d) - 1][: n + 1]
            pick = part if pick is None else jnp.where(index == d, part, pick)
        packed.append(pick)
    return jnp.concatenate(packed)


def gather_inverse(own, low_first):
    part = own_part(own, 0, "col")
    size = lax.axis_size("depth")
    if part.shape[0] % 8:
        return from_columns(from_depth(part, False), low_first)
    part = part.reshape(part.shape[0], size, -1).transpose(1, 0, 2)
    parts = [exchange(part, "depth", k) for k in range(1, size)]
    return from_columns(pack_lower(parts), low_first)


def from_columns(parts, low_first):
    size = lax.axis_size("col")
    bits = [1 << b for b in range(size.bit_length() - 1)]
    known = {0: parts}
    for bit in bits:
        known[bit] = exchange(parts, "col", bit)
    for k in range(1, size):
        if k not in known:
            via = [b for b in (bits if low_first else bits[::-1]) if k & b][-1]
            known[k] = exchange(known[k ^ via], "col", via)
    return [known[k] for k in range(size)]


def gather_factor(own, low_first, relay):
    return from_columns(from_depth(own_part(own, 0, "col"), relay), low_first)


def halves(value):
    high = value.astype(jnp.bfloat16)
    return high, (value - high.astype(jnp.float32)).astype(jnp.bfloat16)


def product(left, right):
    left_high, left_low = halves(left)
    right_high, right_low = right
    dot = functools.partial(jnp.dot, preferred_element_type=jnp.float32)
    return dot(left_high, right_high) + (dot(left_high, right_low) + dot(left_low, right_high))


def solve_kernel(blocks, place, own, *rest):
    *parts, rhs, out = rest
    high, low = halves(rhs[...])
    _, size, width = parts[0].shape
    out[0] = product(own[0], (high, low))
    first = 0
    for n in range(1, blocks):
        chunks = range(first, first + n + 1)
        first += n + 1
        left = jnp.concatenate([jnp.concatenate([part[c] for c in chunks], axis=1) for part in parts])
        depth = (n + 1) * width
        rows = product(left, (high[:depth], low[:depth]))
        source = n - 1 + (n - 1 >= place[2]).astype(jnp.int32)
        for k in range(len(parts)):
            at = pl.multiple_of((place[1] ^ k) * size, size)
            out[source ^ place[2], pl.ds(at, size), :] = rows[k * size : (k + 1) * size]


def update_kernel(quarters, place, *rest):
    *rest, base, out = rest
    sections = (len(rest) - quarters) // 2
    own, parts, solved = rest[:sections], rest[sections : sections + quarters], rest[sections + quarters :]
    count, size, _ = parts[0].shape
    depth = solved[0].shape[1]
    near = far = None
    for s, blocks in enumerate(solved):
        at = slice(s * depth, (s + 1) * depth)
        for j in range(count + 1):
            right = halves(blocks[j])
            if j == 0:
                term = product(own[s][...], right)
                near = term if near is None else near + term
            else:
                left = jnp.concatenate([part[j - 1][:, at] for part in parts])
                term = product(left, right)
                far = term if far is None else far + term
    out[...] = base[...] - near
    for k in range(quarters):
        at = pl.ds(pl.multiple_of((place[1] ^ k) * size, size), size)
        out[at, :] = out[at, :] - far[k * size : (k + 1) * size]


def whole(array):
    zeros = (0,) * array.ndim
    return pl.BlockSpec(array.shape, lambda i, p: zeros)


def cost(flops, arrays):
    moved = sum(4 * a.size for a in arrays)
    return pl.CostEstimate(flops=flops, bytes_accessed=moved, transcendentals=0)


def call_kernel(kernel, place, first_spec, operands, shape, flops):
    out = jax.ShapeDtypeStruct(shape, jnp.float32)
    return pl.pallas_call(
        kernel,
        out_shape=out,
        grid_spec=pltpu.PrefetchScalarGridSpec(
            num_scalar_prefetch=1,
            grid=(1,),
            in_specs=[first_spec] + [whole(a) for a in operands[1:]],
            out_specs=whole(out),
        ),
        cost_estimate=cost(flops, operands[1:]),
        compiler_params=pltpu.CompilerParams(vmem_limit_bytes=24 * 2**20),
    )(place, *operands)


def plain_product(left, right):
    return jnp.dot(left, right, precision=lax.Precision.HIGH, preferred_element_type=jnp.float32)


def solve(place, section, inverses, parts, rhs):
    rows = inverses.shape[1] // lax.axis_size("row")
    nb, cols = rhs.shape
    blocks = nb // inverses.shape[1]
    if (rows // len(parts)) % 8:
        own = plain_product(own_part(inverses[section], 0, "row"), rhs)
        ordered = jnp.concatenate(in_order(list(parts), place[1]), axis=1)
        return jnp.stack([own] + [plain_product(ordered[j], rhs) for j in range(blocks - 1)])
    spec = pl.BlockSpec((1, rows, nb), lambda i, p: (section, p[0], 0))
    shape = (blocks, rows, cols)
    flops = 6 * blocks * rows * nb * cols
    kernel = functools.partial(solve_kernel, blocks)
    return call_kernel(kernel, place, spec, (inverses, *parts, rhs), shape, flops)


def update(place, own, parts, solved, base):
    count, size, _ = parts[0].shape
    depth = solved[0].shape[1]
    if size % 8:
        ordered = jnp.concatenate(in_order(list(parts), place[1]), axis=1)
        for s, blocks in enumerate(solved):
            at = slice(s * depth, (s + 1) * depth)
            base = base - plain_product(own[s], blocks[0])
            for j in range(count):
                base = base - plain_product(ordered[j][:, at], blocks[j + 1])
        return base
    kernel = functools.partial(update_kernel, len(parts))
    flops = 6 * sum(a.size for a in own) * (count + 1) * base.shape[1]
    return call_kernel(kernel, place, whole(own[0]), (*own, *parts, *solved, base), base.shape, flops)


def to_output(parts):
    arrived = [parts[0]]
    for k in range(1, parts.shape[0]):
        arrived.append(exchange(parts[k], "depth", k))
    placed = jnp.concatenate(in_order(arrived, lax.axis_index("depth")), axis=1)
    return share_rows(placed, 0)


def steps(head_rhs, head_factor, inverses, trail_factor, trail_rhs):
    place = jnp.stack([lax.axis_index(axis) for axis in ("row", "col", "depth")])
    lower = own_part(inverses, 1, "row")
    count = trail_factor.shape[0]
    trail_own = [trail_factor[:, section, :] for section in range(trail_factor.shape[1])]
    trail_part = own_part(trail_factor, 0, "col").reshape(count // lax.axis_size("col"), -1)
    first_factor = gather_inverse(lower[0], True)
    mid_factor = gather_factor(head_factor, False, False)
    second_factor = gather_inverse(lower[1], True)
    trail_parts = from_columns(from_depth(trail_part, False), True)

    rhs = share_rows(head_rhs[0], 0)
    first_part = solve(place, 0, inverses, first_factor, rhs)
    first = share_rows(first_part, 1)
    second_rhs = update(place, [head_factor], mid_factor, [first], head_rhs[1])
    second_rhs = share_rows(second_rhs, 0)
    second_part = solve(place, 1, inverses, second_factor, second_rhs)
    second = share_rows(second_part, 1)
    trail_out = update(place, trail_own, trail_parts, [first, second], trail_rhs)
    return jnp.stack([to_output(first_part), to_output(second_part)]), trail_out


def solution(mesh):
    placed = (
        P(None, "row", ("col", "depth")),
        P("row", "depth"),
        P(None, "depth", None),
        P("row", None, "depth"),
        P("row", ("col", "depth")),
    )
    return jax.shard_map(
        steps,
        mesh=mesh,
        in_specs=placed,
        out_specs=(P(None, "depth", "col"), P("row", ("col", "depth"))),
        check_vma=False,
    )
```

```python
import functools

import jax
import jax.numpy as jnp
from jax import lax
from jax.experimental import pallas as pl
from jax.experimental.pallas import tpu as pltpu
from jax.sharding import PartitionSpec as P


def exchange(value, axis, flip):
    pairs = [(i, i ^ flip) for i in range(lax.axis_size(axis))]
    return lax.ppermute(value, axis, pairs)


def in_order(blocks, index):
    bit = 1
    while bit < len(blocks):
        odd = (index & bit) != 0
        blocks = [jnp.where(odd, blocks[k ^ bit], blocks[k]) for k in range(len(blocks))]
        bit *= 2
    return blocks


def share_rows(value, dim):
    index = lax.axis_index("row")
    bit = 1
    while bit < lax.axis_size("row"):
        other = exchange(value, "row", bit)
        odd = (index & bit) != 0
        value = jnp.concatenate([jnp.where(odd, other, value), jnp.where(odd, value, other)], axis=dim)
        bit *= 2
    return value


def own_part(value, dim, axis):
    size = value.shape[dim] // lax.axis_size(axis)
    return lax.dynamic_slice_in_dim(value, lax.axis_index(axis) * size, size, dim)


def from_depth(part):
    size = lax.axis_size("depth")
    known = {}
    for k in range(size - 1, 0, -1):
        if k % 2 == 0:
            known[k] = exchange(known[k + 1], "depth", 1)
        else:
            known[k] = exchange(part, "depth", k)
    return [known[k] for k in range(1, size)]


def pack_lower(parts):
    index = lax.axis_index("depth")
    size = len(parts) + 1
    packed = []
    for n in range(1, size):
        pick = None
        for d in range(size):
            source = n - 1 if n - 1 < d else n
            part = parts[(source ^ d) - 1][: n + 1]
            pick = part if pick is None else jnp.where(index == d, part, pick)
        packed.append(pick)
    return jnp.concatenate(packed)


def gather_inverse(own, low_first):
    part = own_part(own, 0, "col")
    size = lax.axis_size("depth")
    if part.shape[0] % 8:
        return gather_factor(part, low_first)
    part = part.reshape(part.shape[0], size, -1).transpose(1, 0, 2)
    return from_columns(pack_lower(from_depth(part)), low_first)


def from_columns(parts, low_first):
    size = lax.axis_size("col")
    bits = [1 << b for b in range(size.bit_length() - 1)]
    known = {0: parts}
    for bit in bits:
        known[bit] = exchange(parts, "col", bit)
    for k in range(1, size):
        if k not in known:
            via = [b for b in (bits if low_first else bits[::-1]) if k & b][-1]
            known[k] = exchange(known[k ^ via], "col", via)
    return [known[k] for k in range(size)]


def gather_factor(part, low_first):
    return from_columns(jnp.stack(from_depth(part)), low_first)


def halves(value):
    high = value.astype(jnp.bfloat16)
    return high, (value - high.astype(jnp.float32)).astype(jnp.bfloat16)


def product(left, right):
    left_high, left_low = halves(left)
    right_high, right_low = right
    dot = functools.partial(jnp.dot, preferred_element_type=jnp.float32)
    return dot(left_high, right_high) + (dot(left_high, right_low) + dot(left_low, right_high))


def solve_kernel(blocks, place, own, *rest):
    *parts, rhs, out = rest
    high, low = halves(rhs[...])
    _, size, width = parts[0].shape
    out[0] = product(own[0], (high, low))
    first = 0
    for n in range(1, blocks):
        chunks = range(first, first + n + 1)
        first += n + 1
        left = jnp.concatenate([jnp.concatenate([part[c] for c in chunks], axis=1) for part in parts])
        depth = (n + 1) * width
        rows = product(left, (high[:depth], low[:depth]))
        source = n - 1 + (n - 1 >= place[2]).astype(jnp.int32)
        for k in range(len(parts)):
            at = pl.multiple_of((place[1] ^ k) * size, size)
            out[source ^ place[2], pl.ds(at, size), :] = rows[k * size : (k + 1) * size]


def update_kernel(quarters, place, *rest):
    *rest, base, out = rest
    sections = (len(rest) - quarters) // 2
    own, parts, solved = rest[:sections], rest[sections : sections + quarters], rest[sections + quarters :]
    count, size, _ = parts[0].shape
    depth = solved[0].shape[1]
    near = far = None
    for s, blocks in enumerate(solved):
        at = slice(s * depth, (s + 1) * depth)
        for j in range(count + 1):
            right = halves(blocks[j])
            if j == 0:
                term = product(own[s][...], right)
                near = term if near is None else near + term
            else:
                left = jnp.concatenate([part[j - 1][:, at] for part in parts])
                term = product(left, right)
                far = term if far is None else far + term
    out[...] = base[...] - near
    for k in range(quarters):
        at = pl.ds(pl.multiple_of((place[1] ^ k) * size, size), size)
        out[at, :] = out[at, :] - far[k * size : (k + 1) * size]


def whole(array):
    zeros = (0,) * array.ndim
    return pl.BlockSpec(array.shape, lambda i, p: zeros)


def cost(flops, arrays):
    moved = sum(4 * a.size for a in arrays)
    return pl.CostEstimate(flops=flops, bytes_accessed=moved, transcendentals=0)


def call_kernel(kernel, place, first_spec, operands, shape, flops):
    out = jax.ShapeDtypeStruct(shape, jnp.float32)
    return pl.pallas_call(
        kernel,
        out_shape=out,
        grid_spec=pltpu.PrefetchScalarGridSpec(
            num_scalar_prefetch=1,
            grid=(1,),
            in_specs=[first_spec] + [whole(a) for a in operands[1:]],
            out_specs=whole(out),
        ),
        cost_estimate=cost(flops, operands[1:]),
        compiler_params=pltpu.CompilerParams(vmem_limit_bytes=24 * 2**20),
    )(place, *operands)


def plain_product(left, right):
    return jnp.dot(left, right, precision=lax.Precision.HIGH, preferred_element_type=jnp.float32)


def solve(place, section, inverses, parts, rhs):
    rows = inverses.shape[1] // lax.axis_size("row")
    nb, cols = rhs.shape
    blocks = nb // inverses.shape[1]
    if (rows // len(parts)) % 8:
        own = plain_product(own_part(inverses[section], 0, "row"), rhs)
        ordered = jnp.concatenate(in_order(list(parts), place[1]), axis=1)
        return jnp.stack([own] + [plain_product(ordered[j], rhs) for j in range(blocks - 1)])
    spec = pl.BlockSpec((1, rows, nb), lambda i, p: (section, p[0], 0))
    shape = (blocks, rows, cols)
    flops = 6 * blocks * rows * nb * cols
    kernel = functools.partial(solve_kernel, blocks)
    return call_kernel(kernel, place, spec, (inverses, *parts, rhs), shape, flops)


def update(place, own, parts, solved, base):
    count, size, _ = parts[0].shape
    depth = solved[0].shape[1]
    if size % 8:
        ordered = jnp.concatenate(in_order(list(parts), place[1]), axis=1)
        for s, blocks in enumerate(solved):
            at = slice(s * depth, (s + 1) * depth)
            base = base - plain_product(own[s], blocks[0])
            for j in range(count):
                base = base - plain_product(ordered[j][:, at], blocks[j + 1])
        return base
    kernel = functools.partial(update_kernel, len(parts))
    flops = 6 * sum(a.size for a in own) * (count + 1) * base.shape[1]
    return call_kernel(kernel, place, whole(own[0]), (*own, *parts, *solved, base), base.shape, flops)


def to_output(parts):
    arrived = [parts[0]]
    for k in range(1, parts.shape[0]):
        arrived.append(exchange(parts[k], "depth", k))
    placed = jnp.concatenate(in_order(arrived, lax.axis_index("depth")), axis=1)
    return share_rows(placed, 0)


def steps(head_rhs, head_factor, inverses, trail_factor, trail_rhs):
    place = jnp.stack([lax.axis_index(axis) for axis in ("row", "col", "depth")])
    lower = own_part(inverses, 1, "row")
    count = trail_factor.shape[0]
    trail_own = [trail_factor[:, section, :] for section in range(trail_factor.shape[1])]
    trail_part = own_part(trail_factor, 0, "col").reshape(count // lax.axis_size("col"), -1)
    first_factor = gather_inverse(lower[0], True)
    mid_factor = gather_factor(own_part(head_factor, 0, "col"), False)
    second_factor = gather_inverse(lower[1], True)
    trail_parts = gather_factor(trail_part, True)

    rhs = share_rows(head_rhs[0], 0)
    first_part = solve(place, 0, inverses, first_factor, rhs)
    first = share_rows(first_part, 1)
    second_rhs = update(place, [head_factor], mid_factor, [first], head_rhs[1])
    second_rhs = share_rows(second_rhs, 0)
    second_part = solve(place, 1, inverses, second_factor, second_rhs)
    second = share_rows(second_part, 1)
    trail_out = update(place, trail_own, trail_parts, [first, second], trail_rhs)
    return jnp.stack([to_output(first_part), to_output(second_part)]), trail_out


def solution(mesh):
    placed = (
        P(None, "row", ("col", "depth")),
        P("row", "depth"),
        P(None, "depth", None),
        P("row", None, "depth"),
        P("row", ("col", "depth")),
    )
    return jax.shard_map(
        steps,
        mesh=mesh,
        in_specs=placed,
        out_specs=(P(None, "depth", "col"), P("row", ("col", "depth"))),
        check_vma=False,
    )
```
